32 devices in a mesh: groups: 2 (over x), expert: 16 (over z, y, core).
Axes of the slice: x: 2, y: 2, z: 4, core: 2. Of those that a mesh axis runs over, the one named last changes fastest.
Arguments:
- routes: int32 [2, 2048, 8], P(None, ('groups', 'expert')), parts along dimension 1, may hold values from 0 to 31, as said below
- gate_weights: float32 [2, 2048, 8], P(None, ('groups', 'expert')), parts along dimension 1, may hold values from 0.05 to 0.5
- grad_out: bfloat16 [2, 2048, 2048], P(None, ('groups', 'expert')), parts along dimension 1, may hold values from -6 to 6
- saved_hidden: bfloat16 [4, 32, 384, 768], P('groups', 'expert'), parts along dimension 0, may hold values from -20 to 20
- down_weight: bfloat16 [32, 768, 2048], P('expert'), may hold values from -0.21875 to 0.21875
Outputs:
- hidden_grad: bfloat16 [2, 2048, 8, 768], P(None, ('groups', 'expert')), parts along dimension 1
- update: bfloat16 [32, 1536, 2048], P('expert', 'groups'), parts along dimension 1
The draws below stay inside these ranges and needn't reach their ends.
There are 2 independent parts, one for each index of `groups`. The reference program is written for one: setup_inputs(seed, part) draws one part's arguments, and reference() takes and returns one part's arrays. A program takes and returns all parts, laid end to end along the dimension named above; an argument that names none is the same for every part. Nothing has to cross between parts.
Inputs may be any that keep to these rules, and one draw needn't show every extreme that they name: `routes`: each token names 8 different experts. In each micro-batch the 64 tokens of one source name any expert at most 24 times, and some expert exactly 24 times by the tokens of every source.
All inputs are finite; a program needn't handle non-finite values.
Results may differ from the reference program's by a relative error of at most 0.011.
Values may be sent and summed in bfloat16 or wider, within the bound.
No kernel may reach another device: no remote copies, remote signals or barrier semaphores. Data moves between devices by JAX's collectives and lax.ppermute only.
A program may use at most 128 MiB of HBM per device.

```python
import math
import jax
import jax.numpy as jnp
from jax import lax

D = 2048
FF = 768
TOP = 8
MB = 2
TOK_DEV = 64
EXPERTS = 32
TOKENS = 1024
MEAN = 16
CAP = 24
SLOTS = 384
N_EXPERT = 16


def block_routes(block_key, hot_expert):
    sub_keys = jax.random.split(block_key, 3)
    expert_perm = jax.random.permutation(sub_keys[0], EXPERTS).astype(jnp.int32)
    where_hot = jnp.argmax((expert_perm == hot_expert).astype(jnp.int32))
    first_expert = expert_perm[0]
    expert_order = expert_perm.at[where_hot].set(first_expert).at[0].set(hot_expert)
    half_mean = MEAN // 2
    swing_size = jax.random.randint(sub_keys[1], (EXPERTS // 2,), 0, half_mean + 1).astype(jnp.int32)
    swing_size = swing_size.at[0].set(half_mean)
    counts = jnp.stack([MEAN + swing_size, MEAN - swing_size], axis=1).reshape(EXPERTS)
    run_ends = jnp.cumsum(counts)
    pick_index = jnp.arange(TOK_DEV * TOP, dtype=jnp.int32)
    run_rank = jnp.sum((run_ends[None, :] <= pick_index[:, None]).astype(jnp.int32), axis=1)
    chosen = expert_order[run_rank]
    route_table = chosen.reshape(TOP, TOK_DEV).T
    shuffle = jax.random.permutation(sub_keys[2], TOK_DEV)
    return route_table[shuffle]


def draw_routes(key, part):
    hot_expert = jax.random.randint(jax.random.fold_in(key, 7), (), 0, EXPERTS).astype(jnp.int32)
    block_keys = jax.random.split(jax.random.fold_in(key, 11), MB * N_EXPERT)

    def one_block(block_key):
        return block_routes(block_key, hot_expert)
    all_tables = jax.vmap(one_block)(block_keys)
    return all_tables.reshape(MB, N_EXPERT * TOK_DEV, TOP).astype(jnp.int32)


def draw_saved_hidden(key, part):
    sub_keys = jax.random.split(jax.random.fold_in(key, 23), 2)
    shape = (MB, EXPERTS, SLOTS, FF)
    column_scale = jnp.exp(jax.random.uniform(sub_keys[0], (1, EXPERTS, 1, FF), jnp.float32, 0.0, math.log(10.0))) / 3.0
    values = column_scale * jnp.clip(jax.random.normal(sub_keys[1], shape, jnp.float32), -5.0, 5.0)
    return values.astype(jnp.bfloat16)


def shard_levels(stream_key, shape, cuts, low, top_value):
    gain = 1.0
    for axis_at, blocks in cuts:
        heights = jax.random.uniform(jax.random.fold_in(jax.random.fold_in(stream_key, 6), axis_at), (blocks,), jnp.float32, low / len(cuts), top_value / len(cuts))
        gain = gain * jnp.repeat(jnp.exp(heights), shape[axis_at] // blocks).reshape((-1,) + (1,) * (len(shape) - 1 - axis_at))
    return gain


def bell_draw(own_key, dims, scale, reach, cuts=(), kind=jnp.bfloat16):
    gain = shard_levels(own_key, dims, cuts, -0.22, 0.18) if cuts else 1.0
    result = jax.random.normal(own_key, dims, jnp.float32) * scale * gain
    return jnp.minimum(jnp.maximum(result, -reach), reach).astype(kind)


def setup_inputs(seed: int = 0, part: int = 0) -> dict:
    arg_keys = jax.random.split(jax.random.key(seed), 6)
    part_splits = jax.random.split(jax.random.fold_in(arg_keys[5], part), 6)
    routes = draw_routes(jax.random.fold_in(jax.random.fold_in(arg_keys[5], part), 71), part)
    gate_weights = jnp.clip(jnp.exp(math.log(0.5) - 2.3025851 * jax.random.uniform(part_splits[1], (MB, TOKENS, TOP), jnp.float32) ** shard_levels(part_splits[1], (MB, TOKENS, TOP), ((1, 16),), -0.2, 0.2)), 0.05, 0.5)
    grad_out = bell_draw(part_splits[2], (MB, TOKENS, D), 1.0, 6.0, ((1, 16),))
    saved_hidden = draw_saved_hidden(jax.random.fold_in(jax.random.fold_in(arg_keys[5], part), 71), part)
    down_weight = bell_draw(arg_keys[4], (EXPERTS, FF, D), FF ** -0.5, 0.21875, ((0, 16),))
    return {"routes": routes, "gate_weights": gate_weights, "grad_out": grad_out, "saved_hidden": saved_hidden, "down_weight": down_weight}


def orthogonal_step(weight_grad):
    grad_wide = weight_grad.astype(jnp.float32)
    gram_raw = jnp.einsum('efd,egd->efg', grad_wide, grad_wide, precision=lax.Precision.HIGHEST)
    frob_norm = jnp.sqrt(lax.optimization_barrier(jnp.sum(gram_raw * gram_raw, axis=(1, 2)))) + 1e-06
    gram_unit = gram_raw / frob_norm[:, None, None]
    gram_half = gram_unit.astype(jnp.bfloat16).astype(jnp.float32)
    identity = jnp.eye(FF, dtype=jnp.float32)[None]
    square_first = jnp.einsum('efg,egh->efh', gram_half, gram_half, precision=lax.Precision.HIGHEST)
    poly_first = (3.4445 * identity - 4.775 * gram_unit + 2.0315 * square_first).astype(jnp.bfloat16).astype(jnp.float32)
    left_product = jnp.einsum('efg,egh->efh', poly_first, gram_half, precision=lax.Precision.HIGHEST).astype(jnp.bfloat16).astype(jnp.float32)
    gram_next = jnp.einsum('efg,egh->efh', left_product, poly_first, precision=lax.Precision.HIGHEST)
    next_half = gram_next.astype(jnp.bfloat16).astype(jnp.float32)
    square_next = jnp.einsum('efg,egh->efh', next_half, next_half, precision=lax.Precision.HIGHEST)
    poly_next = (3.4445 * identity - 4.775 * gram_next + 2.0315 * square_next).astype(jnp.bfloat16).astype(jnp.float32)
    product = jnp.einsum('efg,egh->efh', poly_next, poly_first, precision=lax.Precision.HIGHEST)
    scaling = math.sqrt(D) / jnp.sqrt(frob_norm)
    combined = (product * scaling[:, None, None]).astype(jnp.bfloat16).astype(jnp.float32)
    return jnp.einsum('efg,egd->efd', combined, grad_wide, precision=lax.Precision.HIGHEST).astype(jnp.bfloat16)

def reference(routes, gate_weights, grad_out, saved_hidden, down_weight):
    blocks = routes.reshape(MB * N_EXPERT, TOK_DEV, TOP)
    matches = (blocks[..., None] == jnp.arange(EXPERTS, dtype=jnp.int32)).astype(jnp.int32)
    per_token = lax.optimization_barrier(jnp.sum(matches, axis=2))
    earlier = jnp.cumsum(per_token, axis=1) - per_token
    slot_index = lax.optimization_barrier(jnp.sum(matches * earlier[:, :, None, :], axis=3)).reshape(MB, TOKENS, TOP)
    source = (jnp.arange(TOKENS, dtype=jnp.int32) // TOK_DEV)[None, :, None]
    column = (source * CAP + slot_index).astype(jnp.int32)
    gated_rows = (gate_weights[..., None] * grad_out[:, :, None, :].astype(jnp.float32)).astype(jnp.bfloat16)
    batch_ids = jnp.broadcast_to(jnp.arange(MB, dtype=jnp.int32)[:, None, None], routes.shape)
    dispatched = jnp.zeros((MB, EXPERTS, SLOTS, D), jnp.bfloat16).at[batch_ids, routes, column].set(gated_rows)
    dispatched_wide = dispatched.astype(jnp.float32)
    slot_grad = jnp.einsum('mesd,efd->mesf', dispatched_wide, down_weight.astype(jnp.float32), precision=lax.Precision.HIGHEST).astype(jnp.bfloat16)
    hidden_grad = slot_grad[batch_ids, routes, column]
    weight_grad = jnp.einsum('mesf,mesd->efd', saved_hidden.astype(jnp.float32), dispatched_wide, precision=lax.Precision.HIGHEST).astype(jnp.bfloat16)
    update = orthogonal_step(weight_grad)
    return (hidden_grad, update)
```

```python
import functools
import math

import jax
import jax.numpy as jnp
import numpy as np
from jax import lax
from jax.experimental import pallas as pl
from jax.experimental.pallas import tpu as pltpu
from jax.sharding import PartitionSpec as P

COEF_A = 3.4445
COEF_B = -4.775
COEF_C = 2.0315
AXIS = "expert"
NT = (((1,), (1,)), ((), ()))


def ring_layout(mesh):
    row = np.asarray(mesh.devices)[0].reshape(-1)
    chips = len(row) // 2
    coords = [getattr(d, "coords", None) for d in row[::2]]
    if any(c is None for c in coords):
        return list(range(chips))
    ys = sorted({c[1] for c in coords})
    if len(ys) != 2:
        return list(range(chips))
    first = [i for i in range(chips) if coords[i][1] == ys[0]]
    second = [i for i in range(chips) if coords[i][1] == ys[1]]
    first.sort(key=lambda i: coords[i][2])
    second.sort(key=lambda i: -coords[i][2])
    return first + second


def shift_pairs(order, step):
    chips = len(order)
    return [
        (order[p] * 2 + core, order[(p + step) % chips] * 2 + core)
        for p in range(chips)
        for core in range(2)
    ]


def swap_pairs(devices):
    return [(i, i ^ 1) for i in range(devices)]


def source_table(order):
    chips = len(order)
    place = {chip: p for p, chip in enumerate(order)}
    table = np.zeros((chips * 2, chips * 2), np.int32)
    for i in range(chips * 2):
        p, core = place[i // 2], i % 2
        steps = [0]
        for s in range(1, chips // 2):
            steps += [-s, s]
        steps.append(chips // 2)
        row = []
        for s in steps:
            chip = order[(p + s) % chips]
            row += [chip * 2 + core, chip * 2 + 1 - core]
        table[i] = row
    return table


def spread_small(value, devices):
    gathered = value[None]
    bit = 1
    while bit < devices:
        other = lax.ppermute(gathered, AXIS, [(i, i ^ bit) for i in range(devices)])
        gathered = jnp.concatenate([gathered, other], axis=0)
        bit *= 2
    return gathered


def expert_kernel(count, first, ids_ref, me_ref, *refs):
    tok_refs = refs[: 2 * count]
    refs = refs[2 * count :]
    if first:
        sel_hbm, gate_hbm, w_hbm, disp_out, grad_out = refs[:5]
        refs = refs[5:]
    else:
        sel_hbm, gate_hbm, w_hbm, _, _, disp_out, grad_out = refs[:7]
        refs = refs[7:]
    tok, sel, gate, w, rows, back, in_sem, w_sem, out_sem = refs
    width = tok.shape[2]
    half = tok.shape[1] // 2
    part = rows.shape[1] // count
    hidden = w.shape[1]
    sources = [ids_ref[i] for i in range(count)]
    slots = [jnp.bitwise_xor(me_ref[0], s) for s in sources]
    loads = []
    for i in range(count):
        loads.append(
            [
                pltpu.make_async_copy(tok_refs[2 * i], tok.at[i, pl.ds(0, half)], in_sem.at[i, 0]),
                pltpu.make_async_copy(tok_refs[2 * i + 1], tok.at[i, pl.ds(half, half)], in_sem.at[i, 1]),
                pltpu.make_async_copy(sel_hbm.at[slots[i]], sel.at[i], in_sem.at[i, 2]),
                pltpu.make_async_copy(gate_hbm.at[slots[i]], gate.at[i], in_sem.at[i, 3]),
            ]
        )
        for c in loads[i]:
            c.start()
    w_loads = [pltpu.make_async_copy(w_hbm.at[e], w.at[e], w_sem.at[e]) for e in range(2)]
    for c in w_loads:
        c.start()
    stores = []
    step = min(512, width)
    for i in range(count):
        for c in loads[i]:
            c.wait()
        for at in range(0, width, step):
            picked = jnp.dot(sel[i], tok[i, :, at : at + step], preferred_element_type=jnp.float32)
            gated = (picked * gate[i]).astype(jnp.bfloat16)
            for e in range(2):
                rows[e, i * part : (i + 1) * part, at : at + step] = gated[e * part : (e + 1) * part]
        for e in range(2):
            c = pltpu.make_async_copy(
                rows.at[e, pl.ds(i * part, part)], disp_out.at[e, sources[i]], out_sem.at[i, e]
            )
            c.start()
            stores.append(c)
    for e in range(2):
        w_loads[e].wait()
        for at in range(0, hidden, 256):
            product = lax.dot_general(
                rows[e], w[e, at : at + 256, :], NT, preferred_element_type=jnp.float32
            ).astype(jnp.bfloat16)
            for i in range(count):
                back[i, e, :, at : at + 256] = product[i * part : (i + 1) * part]
    for i in range(count):
        c = pltpu.make_async_copy(back.at[i], grad_out.at[sources[i]], out_sem.at[i, 2])
        c.start()
        stores.append(c)
    for c in stores:
        c.wait()


def expert_rows(ids, me, chunks, sel, gate, weight, carried):
    devices, part2, tokens = sel.shape
    part = part2 // 2
    hidden, width = weight.shape[1:]
    count = len(chunks)
    operands = []
    for pair in chunks:
        operands += list(pair)
    any_spec = pl.BlockSpec(memory_space=pl.ANY)
    smem = pl.BlockSpec(memory_space=pltpu.SMEM)
    first = carried is None
    args = [ids, me, *operands, sel, gate, weight]
    aliases = {}
    if not first:
        aliases = {len(args): 0, len(args) + 1: 1}
        args += list(carried)
    flops = 2 * count * part2 * (tokens * width + width * hidden)
    moved = weight.size * 2 + count * (tokens * width + part2 * (width + hidden)) * 2
    return pl.pallas_call(
        functools.partial(expert_kernel, count, first),
        out_shape=(
            jax.ShapeDtypeStruct((2, devices, part, width), jnp.bfloat16),
            jax.ShapeDtypeStruct((devices, 2, part, hidden), jnp.bfloat16),
        ),
        in_specs=[smem, smem] + [any_spec] * (len(args) - 2),
        out_specs=(any_spec, any_spec),
        scratch_shapes=[
            pltpu.VMEM((count, tokens, width), jnp.bfloat16),
            pltpu.VMEM((count, part2, tokens), jnp.bfloat16),
            pltpu.VMEM((count, part2, 1), jnp.float32),
            pltpu.VMEM((2, hidden, width), jnp.bfloat16),
            pltpu.VMEM((2, count * part, width), jnp.bfloat16),
            pltpu.VMEM((count, 2, part, hidden), jnp.bfloat16),
            pltpu.SemaphoreType.DMA((count, 4)),
            pltpu.SemaphoreType.DMA((2,)),
            pltpu.SemaphoreType.DMA((count, 3)),
        ],
        input_output_aliases=aliases,
        cost_estimate=pl.CostEstimate(flops=flops, bytes_accessed=moved, transcendentals=0),
        compiler_params=pltpu.CompilerParams(vmem_limit_bytes=40 << 20),
        name=f"expert_rows_{count}",
    )(*args)


def slot_tables(small, me, capacity):
    routes, gates = small[:, 0], small[:, 1]
    devices, batches, top, tokens = routes.shape
    mine = (2 * me + jnp.arange(2)).astype(jnp.float32)
    hit = routes[:, None] == mine[None, :, None, None, None]
    named = jnp.sum(hit.astype(jnp.float32), axis=3)
    gate = jnp.sum(jnp.where(hit, gates[:, None], 0.0), axis=3)
    before = jnp.triu(jnp.ones((tokens, tokens), jnp.float32), 1)
    rank = jnp.einsum("deba,at->debt", named, before)
    slot = jnp.arange(capacity, dtype=jnp.float32)[:, None]
    pick = (rank[:, :, :, None, :] == slot) & (named[:, :, :, None, :] > 0.5)
    row_gate = jnp.sum(jnp.where(pick, gate[:, :, :, None, :], 0.0), axis=4)
    same = jnp.eye(batches, dtype=bool)[None, None, :, None, :, None]
    wide = pick[:, :, :, :, None, :] & same
    rows = 2 * batches * capacity
    return (
        wide.astype(jnp.bfloat16).reshape(devices, rows, batches * tokens),
        row_gate.reshape(devices, rows, 1),
    )


def own_places(routes, experts, capacity):
    matches = (routes[..., None] == jnp.arange(experts, dtype=jnp.int32)).astype(jnp.int32)
    per_token = jnp.sum(matches, axis=2)
    earlier = jnp.cumsum(per_token, axis=1) - per_token
    slot = jnp.sum(matches * earlier[:, :, None, :], axis=3)
    batches = routes.shape[0]
    batch = jnp.arange(batches, dtype=jnp.int32)[:, None, None]
    return (routes * batches + batch) * capacity + slot


def orthogonal_step(weight_grad, model_width):
    hidden_width = weight_grad.shape[1]
    gram_raw = jnp.einsum("efd,egd->efg", weight_grad, weight_grad, preferred_element_type=jnp.float32)
    frob_norm = jnp.sqrt(jnp.sum(gram_raw * gram_raw, axis=(1, 2))) + 1e-06
    gram_unit = gram_raw / frob_norm[:, None, None]
    gram_half = gram_unit.astype(jnp.bfloat16)
    identity = jnp.eye(hidden_width, dtype=jnp.float32)[None]

    def product(a, b):
        return jnp.einsum("efg,egh->efh", a, b, preferred_element_type=jnp.float32)

    square_first = product(gram_half, gram_half)
    poly_first = (COEF_A * identity + COEF_B * gram_unit + COEF_C * square_first).astype(jnp.bfloat16)
    left_product = product(poly_first, gram_half).astype(jnp.bfloat16)
    gram_next = product(left_product, poly_first)
    next_half = gram_next.astype(jnp.bfloat16)
    square_next = product(next_half, next_half)
    poly_next = (COEF_A * identity + COEF_B * gram_next + COEF_C * square_next).astype(jnp.bfloat16)
    scaling = math.sqrt(model_width) / jnp.sqrt(frob_norm)
    combined = (product(poly_next, poly_first) * scaling[:, None, None]).astype(jnp.bfloat16)
    return jnp.einsum("efg,egd->efd", combined, weight_grad, preferred_element_type=jnp.float32).astype(
        jnp.bfloat16
    )


def local(order, routes, gate_weights, grad_out, saved_hidden, down_weight):
    devices = lax.axis_size(AXIS)
    me = lax.axis_index(AXIS)
    chips = devices // 2
    local_experts, hidden, width = down_weight.shape
    batches, tokens, top = routes.shape
    slots = saved_hidden.shape[2]
    capacity = slots // devices
    experts = devices * local_experts
    ahead, behind, swap = shift_pairs(order, 1), shift_pairs(order, -1), swap_pairs(devices)

    def swapped(x):
        return lax.ppermute(x, AXIS, swap)

    small = jnp.stack(
        [jnp.swapaxes(routes, 1, 2).astype(jnp.float32), jnp.swapaxes(gate_weights, 1, 2)]
    )
    groups = [[grad_out]]
    right = left = grad_out
    for step in range(1, chips // 2):
        right = lax.ppermute(right, AXIS, ahead)
        left = lax.ppermute(left, AXIS, behind)
        groups.append([right, left])
    last = (lax.ppermute(right[0], AXIS, ahead), lax.ppermute(left[1], AXIS, behind))
    small = spread_small(small, devices)
    sel, gate = slot_tables(small, me, capacity)
    ids = jnp.asarray(source_table(order))[me]
    me1 = me.reshape(1).astype(jnp.int32)

    carried = None
    done = 0
    for group in groups:
        chunks = []
        for x in group:
            other = swapped(x)
            chunks += [(x[0], x[1]), (other[0], other[1])]
        carried = expert_rows(ids[done : done + len(chunks)], me1, chunks, sel, gate, down_weight, carried)
        done += len(chunks)
    other = (swapped(last[0]), swapped(last[1]))
    carried = expert_rows(ids[done : done + 2], me1, [last, other], sel, gate, down_weight, carried)
    dispatched, slot_grad = carried

    returned = lax.all_to_all(slot_grad, AXIS, split_axis=0, concat_axis=0, tiled=True)

    hidden_rows = saved_hidden.reshape(batches, local_experts, devices, capacity, hidden)
    hidden_rows = jnp.transpose(hidden_rows, (1, 2, 0, 3, 4)).reshape(local_experts, -1, hidden)
    weight_grad = jnp.einsum(
        "jsf,jsd->jfd",
        hidden_rows,
        dispatched.reshape(local_experts, -1, width),
        preferred_element_type=jnp.float32,
    ).astype(jnp.bfloat16)
    update = orthogonal_step(weight_grad, width)

    places = own_places(routes, experts, capacity).reshape(-1, 1)
    table = returned.reshape(-1, hidden)
    chosen = (places == jnp.arange(table.shape[0], dtype=jnp.int32)[None]).astype(jnp.bfloat16)
    hidden_grad = jnp.dot(chosen, table, preferred_element_type=jnp.float32).astype(jnp.bfloat16)
    return hidden_grad.reshape(batches, tokens, top, hidden), update


def solution(mesh):
    in_specs = (
        P(None, ("groups", AXIS), None),
        P(None, ("groups", AXIS), None),
        P(None, ("groups", AXIS), None),
        P("groups", AXIS, None, None),
        P(AXIS, None, None),
    )
    out_specs = (P(None, ("groups", AXIS), None, None), P(AXIS, "groups", None))
    return jax.shard_map(
        functools.partial(local, ring_layout(mesh)),
        mesh=mesh,
        in_specs=in_specs,
        out_specs=out_specs,
        check_vma=False,
    )
```

```python
import functools
import math

import jax
import jax.numpy as jnp
import numpy as np
from jax import lax
from jax.experimental import pallas as pl
from jax.experimental.pallas import tpu as pltpu
from jax.sharding import PartitionSpec as P


COEF_A = 3.4445
COEF_B = -4.775
COEF_C = 2.0315
AXIS = "expert"
META = 8
NN = (((1,), (0,)), ((), ()))
NT = (((1,), (1,)), ((), ()))
TN = (((0,), (0,)), ((), ()))
ANY = pl.BlockSpec(memory_space=pl.ANY)
HBM = pl.BlockSpec(memory_space=pltpu.HBM)
SMEM = pl.BlockSpec(memory_space=pltpu.SMEM)


def ring_layout(mesh):
    row = np.asarray(mesh.devices)[0].reshape(-1)
    chips = len(row) // 2
    coords = [getattr(d, "coords", None) for d in row[::2]]
    if any(c is None for c in coords):
        return list(range(chips))
    ys = sorted({c[1] for c in coords})
    if len(ys) != 2:
        return list(range(chips))
    first = [i for i in range(chips) if coords[i][1] == ys[0]]
    second = [i for i in range(chips) if coords[i][1] == ys[1]]
    first.sort(key=lambda i: coords[i][2])
    second.sort(key=lambda i: -coords[i][2])
    return first + second


def shift_pairs(order, step):
    chips = len(order)
    return [
        (order[p] * 2 + core, order[(p + step) % chips] * 2 + core)
        for p in range(chips)
        for core in range(2)
    ]


def swap_pairs(devices):
    return [(i, i ^ 1) for i in range(devices)]


def source_table(order):
    chips = len(order)
    place = {chip: p for p, chip in enumerate(order)}
    table = np.zeros((chips * 2, chips * 2), np.int32)
    for i in range(chips * 2):
        p, core = place[i // 2], i % 2
        steps = [0]
        for s in range(1, chips // 2):
            steps += [-s, s]
        steps.append(chips // 2)
        row = []
        for s in steps:
            chip = order[(p + s) % chips]
            row += [chip * 2 + core, chip * 2 + 1 - core]
        table[i] = row
    return table


def pack_kernel(routes_ref, gates_ref, tok_ref, out_ref):
    batches, top, tokens = routes_ref.shape
    total = batches * tokens
    width = tok_ref.shape[2]
    for m in range(batches):
        out_ref[m * tokens : (m + 1) * tokens, :] = tok_ref[m]
    routes = jnp.concatenate([routes_ref[m] for m in range(batches)], axis=1).astype(jnp.float32)
    gates = jnp.concatenate([gates_ref[m] for m in range(batches)], axis=1)
    parts = [routes]
    rest = gates
    for _ in range(3):
        part = rest.astype(jnp.bfloat16).astype(jnp.float32)
        parts.append(part)
        rest = rest - part
    parts.append(jnp.zeros((top, width - 4 * total), jnp.float32))
    meta = jnp.concatenate(parts, axis=1)
    out_ref[total : total + META, :] = meta.astype(jnp.bfloat16)


def pack(routes, gates, grad_out):
    batches, tokens, width = grad_out.shape
    return pl.pallas_call(
        pack_kernel,
        out_shape=jax.ShapeDtypeStruct((batches * tokens + META, width), jnp.bfloat16),
        name="pack",
    )(routes, gates, grad_out)


def expert_kernel(pieces, first, batches, ids_ref, me_ref, *refs):
    count = len(pieces)
    chunk_refs = []
    for n in pieces:
        chunk_refs.append(refs[:n])
        refs = refs[n:]
    if first:
        w_hbm, disp_out, grad_out = refs[:3]
        refs = refs[3:]
    else:
        w_hbm, _, _, disp_out, grad_out = refs[:5]
        refs = refs[5:]
    tok, w, rows, back, in_sem, w_sem, out_sem = refs
    width = tok.shape[2]
    total = tok.shape[1] - META
    tokens = total // batches
    part = rows.shape[1] // count
    capacity = part // batches
    hidden = w.shape[1]
    sources = [ids_ref[i] for i in range(count)]
    loads = []
    for i in range(count):
        now, at = [], 0
        for j, ref in enumerate(chunk_refs[i]):
            now.append(pltpu.make_async_copy(ref, tok.at[i, pl.ds(at, ref.shape[0])], in_sem.at[i, j]))
            at += ref.shape[0]
        for c in now:
            c.start()
        loads.append(now)
    w_loads = [pltpu.make_async_copy(w_hbm.at[e], w.at[e], w_sem.at[e]) for e in range(2)]
    for c in w_loads:
        c.start()
    token_at = lax.broadcasted_iota(jnp.int32, (total, total), 0)
    token_to = lax.broadcasted_iota(jnp.int32, (total, total), 1)
    before = ((token_at < token_to) & (token_at // tokens == token_to // tokens)).astype(jnp.bfloat16)
    row = lax.broadcasted_iota(jnp.int32, (part, total), 0)
    lane = lax.broadcasted_iota(jnp.int32, (part, total), 1)
    slot = (row % capacity).astype(jnp.float32)
    same = (row // capacity) == (lane // tokens)
    stores = []
    step = min(512, width)
    for i in range(count):
        for c in loads[i]:
            c.wait()
        meta = tok[i, total:, : 4 * total].astype(jnp.float32)
        routes = meta[:, :total]
        gates = meta[:, total : 2 * total] + meta[:, 2 * total : 3 * total] + meta[:, 3 * total :]
        picks, columns = [], []
        for e in range(2):
            hit = routes == (2 * me_ref[0] + e).astype(jnp.float32)
            named = jnp.sum(jnp.where(hit, 1.0, 0.0), axis=0, keepdims=True)
            gate = jnp.sum(jnp.where(hit, gates, 0.0), axis=0, keepdims=True)
            rank = jnp.dot(
                jnp.broadcast_to(named, (8, total)).astype(jnp.bfloat16),
                before,
                preferred_element_type=jnp.float32,
            )[:1]
            pick = (rank == slot) & (named > 0.5) & same
            picks.append(jnp.where(pick, 1.0, 0.0).astype(jnp.bfloat16))
            columns.append(jnp.sum(jnp.where(pick, gate, 0.0), axis=1, keepdims=True))
        for at in range(0, width, step):
            for e in range(2):
                picked = jnp.dot(picks[e], tok[i, :total, at : at + step], preferred_element_type=jnp.float32)
                rows[e, i * part : (i + 1) * part, at : at + step] = (picked * columns[e]).astype(jnp.bfloat16)
        for e in range(2):
            c = pltpu.make_async_copy(
                rows.at[e, pl.ds(i * part, part)], disp_out.at[e, sources[i]], out_sem.at[i, e]
            )
            c.start()
            stores.append(c)
    for e in range(2):
        w_loads[e].wait()
        for at in range(0, hidden, 256):
            product = lax.dot_general(
                rows[e], w[e, at : at + 256, :], NT, preferred_element_type=jnp.float32
            ).astype(jnp.bfloat16)
            for i in range(count):
                back[i, e, :, at : at + 256] = product[i * part : (i + 1) * part]
    for i in range(count):
        c = pltpu.make_async_copy(back.at[i], grad_out.at[sources[i]], out_sem.at[i, 2])
        c.start()
        stores.append(c)
    for c in stores:
        c.wait()


def expert_rows(ids, me, chunks, weight, carried, devices, batches, capacity):
    operands = [x for pieces in chunks for x in pieces]
    width = weight.shape[2]
    hidden = weight.shape[1]
    part = batches * capacity
    count = len(chunks)
    total = sum(x.shape[0] for x in chunks[0])
    first = carried is None
    args = [ids, me, *operands, weight]
    aliases = {}
    if not first:
        aliases = {len(args): 0, len(args) + 1: 1}
        args += list(carried)
    flops = 4 * count * part * (total * width + width * hidden)
    moved = weight.size * 2 + count * (total * width + 2 * part * (width + hidden)) * 2
    return pl.pallas_call(
        functools.partial(expert_kernel, [len(x) for x in chunks], first, batches),
        out_shape=(
            jax.ShapeDtypeStruct((2, devices, part, width), jnp.bfloat16),
            jax.ShapeDtypeStruct((devices, 2, part, hidden), jnp.bfloat16),
        ),
        in_specs=[SMEM, SMEM] + [ANY] * len(operands) + [HBM] * (len(args) - 2 - len(operands)),
        out_specs=(HBM, HBM),
        scratch_shapes=[
            pltpu.VMEM((count, total, width), jnp.bfloat16),
            pltpu.VMEM((2, hidden, width), jnp.bfloat16),
            pltpu.VMEM((2, count * part, width), jnp.bfloat16),
            pltpu.VMEM((count, 2, part, hidden), jnp.bfloat16),
            pltpu.SemaphoreType.DMA((count, 2)),
            pltpu.SemaphoreType.DMA((2,)),
            pltpu.SemaphoreType.DMA((count, 3)),
        ],
        input_output_aliases=aliases,
        cost_estimate=pl.CostEstimate(flops=flops, bytes_accessed=moved, transcendentals=0),
        compiler_params=pltpu.CompilerParams(vmem_limit_bytes=32 << 20),
    )(*args)


def update_kernel(tile, disp_hbm, hid_hbm, out_hbm, disp, hid, wg, gram, half, poly, left, nxt, out, in_sem, out_sem):
    experts, total, width = disp_hbm.shape
    batches, _, _, _, hidden = hid_hbm.shape
    blocks = hidden // tile
    loads = []
    for e in range(experts):
        now = [pltpu.make_async_copy(disp_hbm.at[e], disp.at[e], in_sem.at[e, 0])]
        for m in range(batches):
            now.append(pltpu.make_async_copy(hid_hbm.at[m, e], hid.at[e, :, m], in_sem.at[e, 1 + m]))
        for c in now:
            c.start()
        loads.append(now)

    def rows(i):
        return pl.ds(pl.multiple_of(i * tile, tile), tile)

    def dot(a, b, dims=NN):
        return lax.dot_general(a, b, dims, preferred_element_type=jnp.float32)

    def diagonal(i):
        r = lax.broadcasted_iota(jnp.int32, (tile, hidden), 0) + i * tile
        return r == lax.broadcasted_iota(jnp.int32, (tile, hidden), 1)

    stores = []
    for e in range(experts):
        for c in loads[e]:
            c.wait()

        @pl.loop(0, blocks)
        def _(i):
            cols = pl.ds(pl.multiple_of(i * tile, tile), tile)
            h = hid[e, :, :, :, cols].reshape(total, tile)
            wg[rows(i), :] = dot(h, disp[e], TN).astype(jnp.bfloat16)

        def gram_rows(i, total_sq):
            g = dot(wg[rows(i), :], wg[...], NT)
            gram[rows(i), :] = g
            return total_sq + jnp.sum(g * g)

        norm = jnp.sqrt(lax.fori_loop(0, blocks, gram_rows, jnp.float32(0.0))) + 1e-06
        half[...] = (gram[...] / norm).astype(jnp.bfloat16)
        scale = COEF_B / norm

        @pl.loop(0, blocks)
        def _(i):
            square = dot(half[rows(i), :], half[...])
            p = COEF_C * square + scale * gram[rows(i), :]
            poly[rows(i), :] = jnp.where(diagonal(i), p + COEF_A, p).astype(jnp.bfloat16)

        @pl.loop(0, blocks)
        def _(i):
            left[rows(i), :] = dot(poly[rows(i), :], half[...]).astype(jnp.bfloat16)

        @pl.loop(0, blocks)
        def _(i):
            g = dot(left[rows(i), :], poly[...])
            gram[rows(i), :] = g
            nxt[rows(i), :] = g.astype(jnp.bfloat16)

        scaling = math.sqrt(width) / jnp.sqrt(norm)

        @pl.loop(0, blocks)
        def _(i):
            square = dot(nxt[rows(i), :], nxt[...])
            p = COEF_C * square + COEF_B * gram[rows(i), :]
            left[rows(i), :] = jnp.where(diagonal(i), p + COEF_A, p).astype(jnp.bfloat16)

        @pl.loop(0, blocks)
        def _(i):
            half[rows(i), :] = (dot(left[rows(i), :], poly[...]) * scaling).astype(jnp.bfloat16)

        @pl.loop(0, blocks)
        def _(i):
            out[e, rows(i), :] = dot(half[rows(i), :], wg[...]).astype(jnp.bfloat16)

        c = pltpu.make_async_copy(out.at[e], out_hbm.at[e], out_sem.at[e])
        c.start()
        stores.append(c)
    for c in stores:
        c.wait()


def expert_update(dispatched, saved_hidden, tile=768):
    experts, total, width = dispatched.shape
    batches, _, sources, capacity, hidden = saved_hidden.shape
    flops = 2 * experts * hidden * (width * (total + 2 * hidden) + 5 * hidden * hidden)
    moved = experts * (total * (width + hidden) + hidden * width) * 2
    square = (hidden, hidden)
    return pl.pallas_call(
        functools.partial(update_kernel, tile),
        out_shape=jax.ShapeDtypeStruct((experts, hidden, width), jnp.bfloat16),
        in_specs=[HBM, ANY],
        out_specs=HBM,
        scratch_shapes=[
            pltpu.VMEM((experts, total, width), jnp.bfloat16),
            pltpu.VMEM((experts, sources, batches, capacity, hidden), jnp.bfloat16),
            pltpu.VMEM((hidden, width), jnp.bfloat16),
            pltpu.VMEM(square, jnp.float32),
            pltpu.VMEM(square, jnp.bfloat16),
            pltpu.VMEM(square, jnp.bfloat16),
            pltpu.VMEM(square, jnp.bfloat16),
            pltpu.VMEM(square, jnp.bfloat16),
            pltpu.VMEM((experts, hidden, width), jnp.bfloat16),
            pltpu.SemaphoreType.DMA((experts, 1 + batches)),
            pltpu.SemaphoreType.DMA((experts,)),
        ],
        cost_estimate=pl.CostEstimate(flops=flops, bytes_accessed=moved, transcendentals=0),
        compiler_params=pltpu.CompilerParams(vmem_limit_bytes=48 << 20),
        name="expert_update",
    )(dispatched, saved_hidden)


def own_places(routes, experts, capacity):
    matches = (routes[..., None] == jnp.arange(experts, dtype=jnp.int32)).astype(jnp.int32)
    per_token = jnp.sum(matches, axis=2)
    earlier = jnp.cumsum(per_token, axis=1) - per_token
    slot = jnp.sum(matches * earlier[:, :, None, :], axis=3)
    batches = routes.shape[0]
    batch = jnp.arange(batches, dtype=jnp.int32)[:, None, None]
    return (routes * batches + batch) * capacity + slot


def local(order, routes, gate_weights, grad_out, saved_hidden, down_weight):
    devices = lax.axis_size(AXIS)
    me = lax.axis_index(AXIS)
    chips = devices // 2
    local_experts, hidden, width = down_weight.shape
    batches, tokens, top = routes.shape
    capacity = saved_hidden.shape[2] // devices
    experts = devices * local_experts
    ahead, behind, swap = shift_pairs(order, 1), shift_pairs(order, -1), swap_pairs(devices)

    def swapped(x):
        return lax.ppermute(x, AXIS, swap)

    chunk = pack(jnp.swapaxes(routes, 1, 2), jnp.swapaxes(gate_weights, 1, 2), grad_out)
    ids = jnp.asarray(source_table(order))[me]
    me1 = me.reshape(1).astype(jnp.int32)
    half = chips // 2
    right = left = chunk
    arrived = [[chunk]]
    for step in range(1, half + 1):
        right = lax.ppermute(right if step < half else right[:tokens], AXIS, ahead)
        left = lax.ppermute(left if step < half else left[tokens:], AXIS, behind)
        arrived.append([right, left])
    carried = None
    done = 0
    waiting = []
    for step, group in enumerate(arrived):
        others = []
        for x in group:
            others.append(swapped(x))
        if step < half:
            waiting += [(c,) for pair in zip(group, others) for c in pair]
        else:
            waiting += [tuple(group), tuple(others)]
        if step == half - 1:
            continue
        carried = expert_rows(
            ids[done : done + len(waiting)], me1, waiting, down_weight, carried, devices, batches, capacity
        )
        done += len(waiting)
        waiting = []
    dispatched, slot_grad = carried

    returned = lax.all_to_all(slot_grad, AXIS, split_axis=0, concat_axis=0, tiled=True)

    update = expert_update(
        dispatched.reshape(local_experts, -1, width),
        saved_hidden.reshape(batches, local_experts, devices, capacity, hidden),
    )

    places = own_places(routes, experts, capacity).reshape(-1, 1)
    table = returned.reshape(-1, hidden)
    chosen = (places == jnp.arange(table.shape[0], dtype=jnp.int32)[None]).astype(jnp.bfloat16)
    hidden_grad = jnp.dot(chosen, table, preferred_element_type=jnp.float32).astype(jnp.bfloat16)
    return hidden_grad.reshape(batches, tokens, top, hidden), update


def solution(mesh):
    in_specs = (
        P(None, ("groups", AXIS), None),
        P(None, ("groups", AXIS), None),
        P(None, ("groups", AXIS), None),
        P("groups", AXIS, None, None),
        P(AXIS, None, None),
    )
    out_specs = (P(None, ("groups", AXIS), None, None), P(AXIS, "groups", None))
    order = ring_layout(mesh)

    def body(*args):
        return local(order, *args)

    return jax.shard_map(body, mesh=mesh, in_specs=in_specs, out_specs=out_specs, check_vma=False)
```
